512 devices in a mesh: sys: 32 (over y_hi, z, core), graph: 16 (over y_lo, x).
Axes of the slice: x: 4, y: 8 (y_hi: 2, y_lo: 4; y = y_hi * 4 + y_lo), z: 8, core: 2. Of those that a mesh axis runs over, the one named last changes fastest.
Arguments:
- node_features: bfloat16 [32, 256, 25, 128], P('sys', 'graph'), may hold values from -6 to 6
- atom_slot: int32 [32, 256], P('sys'), may hold values from 0 to 255, each once within a row
- neighbour: int32 [32, 18432], P('sys', 'graph'), may hold values from 0 to 255
- pad_mask: int32 [32, 18432], P('sys', 'graph'), may hold values 0 or 1
- envelope: float32 [32, 18432], P('sys', 'graph'), may hold values from 0.1 to 1
- wigner_rows: bfloat16 [32, 13, 25, 18432], P('sys', None, None, 'graph'), may hold values from -1.1953125 to 1.1953125
- mix_table: float32 [32, 32], replicated, may hold values from 0.1 to 2
- zero_weight: bfloat16 [32, 640, 640], P('sys', 'graph'), may hold values from -0.0390625 to 0.0390625
- one_weight: bfloat16 [32, 512, 2, 512], P('sys', 'graph'), may hold values from -0.03125 to 0.03125
Outputs:
- update: bfloat16 [32, 256, 25, 128], P('sys', 'graph')
The draws below stay inside these ranges and needn't reach their ends.
Inputs may be any that keep to these rules, and one draw needn't show every extreme that they name: `neighbour`: atom ids of the edge's own system; edge slots a * 72 to a * 72 + 71 belong to the atom in row a of node_features. `atom_slot`: each system's row names every row of node_features once.
All inputs are finite; a program needn't handle non-finite values. No bound on the sum of `pad_mask` on one device may be relied on, other than what follows from the above.
Results may differ from the reference program's by a relative error of at most 0.025.
Values may be sent and summed in bfloat16 or wider, within the bound.
No kernel may reach another device: no remote copies, remote signals or barrier semaphores. Data moves between devices by JAX's collectives and lax.ppermute only.
A program may use at most 64 MiB of HBM per device.

```python
import math
import jax
import jax.numpy as jnp
from jax import lax

C = 128
LMAX = 4
NEIGH = 72
SH = 25
FRAME = 13
M0 = 640
M1 = 512
EXPERTS = 32
SYSTEMS = 32
ATOMS = 256
EDGES = 18432


def touch_ends(entries, own_key, low, top_value):
    spot = [jax.random.randint(jax.random.fold_in(own_key, axis), (), 0, length) for axis, length in enumerate(entries.shape)]
    widest = entries.shape.index(max(entries.shape))
    beside = spot[:widest] + [(spot[widest] + 1) % entries.shape[widest]] + spot[widest + 1:]
    return entries.at[tuple(spot)].set(low).at[tuple(beside)].set(top_value)


def shard_levels(stream_key, dims, shards, smallest, high):
    def one(axis_at, parts):
        heights = jax.random.uniform(jax.random.fold_in(jax.random.fold_in(stream_key, 6), axis_at), (parts,), jnp.float32, smallest / len(shards), high / len(shards))
        return jnp.repeat(jnp.exp(heights), dims[axis_at] // parts).reshape((-1,) + (1,) * (len(dims) - axis_at - 1))

    loudness = one(*shards[0])
    for cut in shards[1:]:
        loudness = loudness * one(*cut)
    return loudness


def gaussian(key, shape, deviation, bound, split=(), held_as=jnp.bfloat16):
    loudness = shard_levels(key, shape, split, -0.22, 0.18) if split else 1.0
    array = jax.random.normal(key, shape, jnp.float32) * deviation * loudness
    return jnp.minimum(jnp.maximum(array, -bound), bound).astype(held_as)


def setup_inputs(seed: int = 0) -> dict:
    arg_keys = jax.random.split(jax.random.key(seed), 10)
    return {
        "node_features": gaussian(arg_keys[0], (SYSTEMS, ATOMS, SH, C), 1.0, 6.0, ((0, 32), (1, 16))),
        "atom_slot": jax.vmap(lambda own: jax.random.permutation(own, ATOMS))(jax.random.split(arg_keys[1], SYSTEMS)).reshape((SYSTEMS, ATOMS)).astype(jnp.int32),
        "neighbour": touch_ends(jax.random.randint(arg_keys[2], (SYSTEMS, EDGES), 0, ATOMS), jax.random.fold_in(arg_keys[2], 1), 0, ATOMS - 1).astype(jnp.int32),
        "pad_mask": touch_ends((jax.random.randint(arg_keys[3], (SYSTEMS, EDGES), 0, 8) < 7).astype(jnp.int32), jax.random.fold_in(arg_keys[3], 1), 0, 1),
        "envelope": jnp.clip(jnp.exp(math.log(1.0) - 2.3025851 * jax.random.uniform(arg_keys[4], (SYSTEMS, EDGES), jnp.float32) ** shard_levels(arg_keys[4], (SYSTEMS, EDGES), ((0, 32), (1, 16)), -0.2, 0.2)), 0.1, 1.0),
        "wigner_rows": gaussian(arg_keys[5], (SYSTEMS, FRAME, SH, EDGES), 0.2, 1.1953125, ((0, 32), (3, 16))),
        "mix_table": jnp.clip(jnp.exp(jax.random.uniform(arg_keys[6], (SYSTEMS, EXPERTS), jnp.float32, math.log(0.1), math.log(2.0))), 0.1, 2.0),
        "zero_weight": gaussian(arg_keys[7], (EXPERTS, M0, M0), (M0 * EXPERTS) ** -0.5, 0.0390625, ((0, 32), (1, 16))),
        "one_weight": gaussian(arg_keys[8], (EXPERTS, M1, 2, M1), (2 * M1 * EXPERTS) ** -0.5, 0.03125, ((0, 32), (1, 16))),
    }


def scaled_term(factor, weight):
    term = (factor * weight.astype(jnp.float32)).astype(jnp.bfloat16)
    term = lax.optimization_barrier(term)
    return term.astype(jnp.float32)

def one_system(inputs):
    features, slots, neighbour, pad_mask, envelope, wigner, merged_zero, merged_one = inputs
    source = jnp.take(slots, neighbour, axis=0)
    gathered = jnp.take(features, source, axis=0)
    rotated = jnp.einsum('rke,ekc->erc', wigner.astype(jnp.float32), gathered.astype(jnp.float32)).astype(jnp.bfloat16)
    edge_count = rotated.shape[0]
    channels = rotated.shape[2]
    first = rotated[:, :LMAX + 1].reshape(edge_count, -1)
    plus_part = rotated[:, LMAX + 1:2 * LMAX + 1].reshape(edge_count, -1)
    minus_part = rotated[:, 2 * LMAX + 1:].reshape(edge_count, -1)
    edge_gate = envelope * pad_mask.astype(jnp.float32)
    real_part = merged_one[:, 0, :]
    imag_part = merged_one[:, 1, :]
    out_zero = jnp.dot(first, merged_zero.T, preferred_element_type=jnp.float32)
    out_plus = jnp.dot(plus_part, real_part.T, preferred_element_type=jnp.float32) - jnp.dot(minus_part, imag_part.T, preferred_element_type=jnp.float32)
    out_minus = jnp.dot(plus_part, imag_part.T, preferred_element_type=jnp.float32) + jnp.dot(minus_part, real_part.T, preferred_element_type=jnp.float32)
    out_zero = (edge_gate[:, None] * out_zero).astype(jnp.bfloat16)
    out_plus = (edge_gate[:, None] * out_plus).astype(jnp.bfloat16)
    out_minus = (edge_gate[:, None] * out_minus).astype(jnp.bfloat16)
    message = jnp.concatenate([out_zero.reshape(edge_count, LMAX + 1, channels), out_plus.reshape(edge_count, LMAX, channels), out_minus.reshape(edge_count, LMAX, channels)], axis=1)
    atom_count = edge_count // NEIGH
    total = jnp.einsum('rkaj,ajrc->akc', wigner.astype(jnp.float32).reshape(wigner.shape[0], wigner.shape[1], atom_count, NEIGH), message.astype(jnp.float32).reshape(atom_count, NEIGH, message.shape[1], channels))
    return (total * (1.0 / math.sqrt(NEIGH))).astype(jnp.bfloat16)

def reference(node_features, atom_slot, neighbour, pad_mask, envelope, wigner_rows, mix_table, zero_weight, one_weight):
    systems = mix_table.shape[0]

    def add_expert(totals, inputs):
        weight_zero, weight_one, column = inputs
        total_zero, total_one = totals
        total_zero = total_zero + scaled_term(column[:, None, None], weight_zero[None])
        total_one = total_one + scaled_term(column[:, None, None, None], weight_one[None])
        return ((total_zero, total_one), None)
    start = (jnp.zeros((systems,) + zero_weight.shape[1:], jnp.float32), jnp.zeros((systems,) + one_weight.shape[1:], jnp.float32))
    (merged_zero, merged_one), _ = lax.scan(add_expert, start, (zero_weight, one_weight, mix_table.T))
    merged_zero = merged_zero.astype(jnp.bfloat16)
    merged_one = merged_one.astype(jnp.bfloat16)
    return lax.map(one_system, (node_features, atom_slot, neighbour, pad_mask, envelope, wigner_rows, merged_zero, merged_one))
```

```python
import math

import jax
import jax.numpy as jnp
from jax import lax
from jax.experimental import pallas as pl
from jax.experimental.pallas import tpu as pltpu
from jax.sharding import Mesh
from jax.sharding import PartitionSpec as P


LMAX = 4
NEIGH = 72
SYS = ("yh", "z", "c")
GRAPH = ("yl", "x")
LANES = 128
PAD = 32
GROUP = 8
MIB = 1024 * 1024


def turned(value, axis, by):
    size = lax.axis_size(axis)
    return lax.ppermute(value, axis, [(i, (i + by) % size) for i in range(size)])


def copies_from_all(value, axis):
    size = math.prod(lax.axis_size(a) for a in axis) if isinstance(axis, tuple) else lax.axis_size(axis)
    spread = jnp.broadcast_to(value[None], (size, *value.shape))
    return lax.all_to_all(spread, axis, 0, 0, tiled=True)


def lane_tiles(rows):
    height, width = rows.shape
    return rows.reshape(height // 8, 8, width // LANES, LANES).transpose(0, 2, 1, 3).reshape(-1, LANES)


def merge_kernel(factor_ref, chunk_ref, send_ref, other_ref, own_ref):
    zs, tiles = chunk_ref.shape[:2]
    targets = (
        (own_ref, [factor_ref[0, k] for k in range(zs)]),
        (send_ref.at[0], [factor_ref[1, k] for k in range(zs)]),
        (other_ref, [factor_ref[2, k] for k in range(zs)]),
        (send_ref.at[1], [factor_ref[3, k] for k in range(zs)]),
    )
    for j in range(tiles):
        pieces = [chunk_ref[k, j].astype(jnp.float32) for k in range(zs)]
        for ref, by in targets:
            total = by[0] * pieces[0]
            for k in range(1, zs):
                total = total + by[k] * pieces[k]
            ref[j] = total.astype(ref.dtype)


def partial_sums(factors, chunks):
    zs, rows, lanes = chunks.shape
    tiles = rows // 8
    one = jax.ShapeDtypeStruct((tiles, 8, lanes), jnp.bfloat16)
    vmem = pl.BlockSpec(memory_space=pltpu.VMEM)
    smem = pl.BlockSpec(memory_space=pltpu.SMEM)
    outs = pl.pallas_call(
        merge_kernel,
        out_shape=(jax.ShapeDtypeStruct((2, tiles, 8, lanes), jnp.bfloat16), one, one),
        in_specs=[smem, vmem],
        out_specs=(vmem, vmem, vmem),
        compiler_params=pltpu.CompilerParams(vmem_limit_bytes=12 * MIB),
        name="merge_experts",
    )(factors, chunks.reshape(zs, tiles, 8, lanes))
    return tuple(o.reshape(-1, rows, lanes) if o.ndim == 4 else o.reshape(rows, lanes) for o in outs)


def rotate_kernel(slot_ref, neighbour_ref, *refs):
    piece_refs = refs[:4]
    wigner_ref, out_ref, feature_ref, spread_ref = refs[4:]
    frame = wigner_ref.shape[0]
    atoms, harmonics = piece_refs[0].shape[:2]
    for k, ref in enumerate(piece_refs):
        feature_ref[k * atoms : (k + 1) * atoms, :harmonics] = ref[...]
    feature_ref[:, harmonics:] = jnp.zeros_like(feature_ref[:, harmonics:])
    width = GROUP * PAD
    block = LANES
    column = lax.broadcasted_iota(jnp.int32, (PAD, width), 1)
    row = lax.broadcasted_iota(jnp.int32, (PAD, width), 0)
    repeat = (column % PAD == row).astype(jnp.bfloat16)
    edge = lax.broadcasted_iota(jnp.int32, (block, width), 0)
    lane = lax.broadcasted_iota(jnp.int32, (block, width), 1)
    own = edge % GROUP == lane // PAD

    def one_block(b, carry):
        start = pl.multiple_of(b * block, block)
        for r in range(frame):
            part = lax.dot_general(
                wigner_ref[r, :, pl.ds(start, block)],
                repeat,
                (((0,), (0,)), ((), ())),
                preferred_element_type=jnp.float32,
            )
            spread_ref[r] = jnp.where(own, part, 0.0)
        for pair in range(block // (2 * GROUP)):
            halves = []
            for half in range(2):
                low = (2 * pair + half) * GROUP
                tiles = []
                for e in range(GROUP):
                    source = slot_ref[neighbour_ref[start + low + e]]
                    tiles.append(feature_ref[source])
                stacked = jnp.concatenate(tiles, axis=0)
                rows = jnp.concatenate(
                    [spread_ref[r, low : low + GROUP, :] for r in range(frame)], axis=0
                ).astype(jnp.bfloat16)
                halves.append(
                    lax.dot_general(
                        rows, stacked, (((1,), (0,)), ((), ())), preferred_element_type=jnp.float32
                    )
                )
            for r in range(frame):
                both = jnp.concatenate([h[GROUP * r : GROUP * (r + 1)] for h in halves], axis=0)
                out_ref[
                    pl.ds(pl.multiple_of(start + 2 * GROUP * pair, 2 * GROUP), 2 * GROUP),
                    r * LANES : (r + 1) * LANES,
                ] = both.astype(out_ref.dtype)
        return carry

    lax.fori_loop(0, neighbour_ref.shape[0] // block, one_block, 0)


def rotate(slots, neighbour, pieces, wigner):
    frame, _, edges = wigner.shape
    atoms = len(pieces) * pieces[0].shape[0]
    return pl.pallas_call(
        rotate_kernel,
        out_shape=jax.ShapeDtypeStruct((edges, frame * LANES), jnp.bfloat16),
        in_specs=[
            pl.BlockSpec(memory_space=pltpu.SMEM),
            pl.BlockSpec(memory_space=pltpu.SMEM),
        ]
        + [pl.BlockSpec(memory_space=pltpu.VMEM)] * (len(pieces) + 1),
        out_specs=pl.BlockSpec(memory_space=pltpu.VMEM),
        scratch_shapes=[
            pltpu.VMEM((atoms, PAD, LANES), jnp.bfloat16),
            pltpu.VMEM((frame, LANES, GROUP * PAD), jnp.float32),
        ],
        compiler_params=pltpu.CompilerParams(vmem_limit_bytes=20 * MIB),
        name="rotate_edges",
    )(slots, neighbour, *pieces, wigner)


def convolve_kernel(zero_shape, one_shape, x_ref, *refs):
    xs = 4
    column_refs = refs[:xs]
    rotated_ref, wigner_ref, out_ref, zero32, one32, zero16, real16, imag16, message, total = refs[xs:]
    zero_rows, zero_width = zero_shape
    parts, one_rows, one_width = one_shape
    ys = column_refs[0].shape[0]
    zero_tiles, one_tiles = zero_width // LANES, one_width // LANES
    for k in range(xs):
        place = (x_ref[1] + k) % xs
        for y in range(ys):
            g = (x_ref[0] + y) % ys * xs + place
            for i in range(zero_rows // 8):
                at = pl.multiple_of(g * zero_rows + 8 * i, 8)
                for t in range(zero_tiles):
                    zero32[pl.ds(at, 8), t * LANES : (t + 1) * LANES] = column_refs[k][
                        y, i * zero_tiles + t
                    ].astype(jnp.float32)
            first = zero_rows // 8 * zero_tiles
            for p in range(parts):
                for i in range(one_rows // 8):
                    at = pl.multiple_of(g * one_rows + 8 * i, 8)
                    for t in range(one_tiles):
                        one32[p, pl.ds(at, 8), t * LANES : (t + 1) * LANES] = column_refs[k][
                            y, first + (p * (one_rows // 8) + i) * one_tiles + t
                        ].astype(jnp.float32)
    zero16[...] = zero32[...].astype(jnp.bfloat16)
    real16[...] = one32[0].astype(jnp.bfloat16)
    imag16[...] = one32[1].astype(jnp.bfloat16)

    edges = rotated_ref.shape[0]
    frame = wigner_ref.shape[0]
    atoms = edges // NEIGH
    side = LMAX * LANES
    near = zero_width

    def times(a, b_ref):
        return lax.dot_general(a, b_ref[...], (((1,), (1,)), ((), ())), preferred_element_type=jnp.float32)

    rows = edges // 3
    for b in range(3):
        span = slice(b * rows, (b + 1) * rows)
        message[span, :near] = times(rotated_ref[span, :near], zero16).astype(jnp.bfloat16)
        plus = rotated_ref[span, near : near + side]
        minus = rotated_ref[span, near + side :]
        message[span, near : near + side] = (times(plus, real16) - times(minus, imag16)).astype(jnp.bfloat16)
        message[span, near + side :] = (times(plus, imag16) + times(minus, real16)).astype(jnp.bfloat16)

    total[...] = jnp.zeros_like(total)
    lane = lax.broadcasted_iota(jnp.int32, (PAD, LANES), 1)
    for b in range(edges // LANES):
        low = b * LANES
        first_atom = low // NEIGH
        last_atom = (low + LANES - 1) // NEIGH
        part = None
        for r0 in range(0, frame, 2):
            pair = [r for r in (r0, r0 + 1) if r < frame]
            left = []
            for r in pair:
                w = wigner_ref[r, :, low : low + LANES]
                picks = []
                for a in range(first_atom, last_atom + 1):
                    inside = (lane + low >= a * NEIGH) & (lane + low < (a + 1) * NEIGH)
                    picks.append(jnp.where(inside, w, jnp.zeros_like(w)))
                left.append(jnp.concatenate(picks, axis=0))
            lhs = jnp.concatenate(left, axis=1)
            rhs = jnp.concatenate(
                [message[low : low + LANES, r * LANES : (r + 1) * LANES] for r in pair], axis=0
            )
            got = lax.dot_general(lhs, rhs, (((1,), (0,)), ((), ())), preferred_element_type=jnp.float32)
            part = got if part is None else part + got
        window = slice(first_atom * PAD, (last_atom + 1) * PAD)
        total[window, :] = total[window, :] + part
    for k in range(out_ref.shape[0]):
        row = total[pl.ds(k, atoms, stride=PAD), :]
        out_ref[k] = (row * (1.0 / math.sqrt(NEIGH))).astype(out_ref.dtype)


def convolve(x, columns, rotated, wigner, zero_shape, one_shape, harmonics):
    edges = rotated.shape[0]
    atoms = edges // NEIGH
    parts, _, one_width = one_shape
    total_zero, total_one = zero_shape[1], one_width
    return pl.pallas_call(
        lambda *refs: convolve_kernel(zero_shape, one_shape, *refs),
        out_shape=jax.ShapeDtypeStruct((harmonics, atoms, LANES), jnp.bfloat16),
        in_specs=[pl.BlockSpec(memory_space=pltpu.SMEM)]
        + [pl.BlockSpec(memory_space=pltpu.VMEM)] * (len(columns) + 2),
        out_specs=pl.BlockSpec(memory_space=pltpu.VMEM),
        scratch_shapes=[
            pltpu.VMEM((total_zero, total_zero), jnp.float32),
            pltpu.VMEM((parts, total_one, total_one), jnp.float32),
            pltpu.VMEM((total_zero, total_zero), jnp.bfloat16),
            pltpu.VMEM((total_one, total_one), jnp.bfloat16),
            pltpu.VMEM((total_one, total_one), jnp.bfloat16),
            pltpu.VMEM((edges, rotated.shape[1]), jnp.bfloat16),
            pltpu.VMEM((atoms * PAD, LANES), jnp.float32),
        ],
        compiler_params=pltpu.CompilerParams(vmem_limit_bytes=28 * MIB),
        name="convolve_edges",
    )(x, *columns, rotated, wigner)


def added(a, b):
    return (a.astype(jnp.float32) + b.astype(jnp.float32)).astype(jnp.bfloat16)


def shards(
    node_features,
    atom_slot,
    neighbour,
    pad_mask,
    envelope,
    wigner_rows,
    mix_table,
    zero_weight,
    one_weight,
):
    yh, z, c = (lax.axis_index(a) for a in SYS)
    y, x = (lax.axis_index(a) for a in GRAPH)
    ys, xs = lax.axis_size("yl"), lax.axis_size("x")
    zero_rows, zero_width = zero_weight.shape[1:]
    one_rows, parts, one_width = one_weight.shape[1:]
    harmonics = wigner_rows.shape[2]
    packed = jnp.concatenate(
        [
            lane_tiles(zero_weight[0]),
            lane_tiles(one_weight[0].transpose(1, 0, 2).reshape(parts * one_rows, one_width)),
        ],
        axis=0,
    )
    chunks = copies_from_all(packed, "z")
    mine = node_features[0].reshape(-1, LANES)
    line = [mine]
    for k in range(1, ys):
        line.append(turned(mine, "yl", -k))
    line = jnp.concatenate(line, axis=0)
    plane = [line]
    for k in range(1, xs):
        plane.append(turned(line, "x", -k))

    edge_gate = envelope[0] * pad_mask[0].astype(jnp.float32)
    padding = ((0, 0), (0, PAD - harmonics), (0, 0))
    wigner = jnp.pad(wigner_rows[0], padding)
    gated = jnp.pad((wigner_rows[0].astype(jnp.float32) * edge_gate).astype(jnp.bfloat16), padding)
    slots = atom_slot[0]
    atoms = node_features.shape[1]
    slots = (
        (slots // atoms - x) % xs * (ys * atoms) + (slots // (xs * atoms) - y) % ys * atoms + slots % atoms
    )
    edges_from = neighbour[0]
    zs = lax.axis_size("z")
    table = mix_table.reshape(2, zs, 2, 2, zs, 2)
    table = lax.dynamic_slice(table, (0, z, 0, yh, 0, c), (2, 1, 2, 1, zs, 1)).reshape(2, 2, zs)
    table = jnp.where(yh == 0, table, table[::-1])
    factors = jnp.where(c == 0, table, table[:, ::-1]).reshape(4, zs)
    there = jnp.stack([y, x])
    wigner, gated, slots, edges_from, chunks, factors, there = lax.optimization_barrier(
        (wigner, gated, slots, edges_from, chunks, factors, there)
    )
    send, other, own = partial_sums(factors, chunks)
    swapped = turned(send, "c", 1)
    outgoing = added(other, swapped[1])
    arrived = turned(outgoing, "yh", 1)
    pieces = [p.reshape(-1, harmonics, LANES) for p in plane]
    arrived, pieces = lax.optimization_barrier((arrived, pieces))
    merged = added(added(own, swapped[0]), arrived)
    column = [merged]
    for k in range(1, ys):
        column.append(turned(merged, "yl", -k))
    column = jnp.stack(column)
    columns = [column]
    for k in range(1, xs):
        columns.append(turned(column, "x", -k))
    rotated = rotate(slots, edges_from, pieces, wigner)
    update = convolve(
        there,
        [m.reshape(ys, -1, 8, LANES) for m in columns],
        rotated,
        gated,
        (zero_rows, zero_width),
        (parts, one_rows, one_width),
        harmonics,
    )
    return update.transpose(1, 0, 2)[None]


def solution(mesh):
    finer = Mesh(mesh.devices.reshape(2, 8, 2, 4, 4), SYS + GRAPH)
    return jax.shard_map(
        shards,
        mesh=finer,
        in_specs=(
            P(SYS, GRAPH, None, None),
            P(SYS, None),
            P(SYS, GRAPH),
            P(SYS, GRAPH),
            P(SYS, GRAPH),
            P(SYS, None, None, GRAPH),
            P(),
            P(SYS, GRAPH, None),
            P(SYS, GRAPH, None, None),
        ),
        out_specs=P(SYS, GRAPH, None, None),
        check_vma=False,
    )
```

```python
import math

import jax
import jax.numpy as jnp
from jax import lax
from jax.experimental import pallas as pl
from jax.experimental.pallas import tpu as pltpu
from jax.sharding import Mesh
from jax.sharding import PartitionSpec as P


LMAX = 4
NEIGH = 72
SYS = ("yh", "z", "c")
GRAPH = ("yl", "x")
LANES = 128
PAD = 32
GROUP = 8
FAR_FIRST = (2, 1, 3)
MIB = 1024 * 1024


def turned(value, axis, by):
    size = lax.axis_size(axis)
    return lax.ppermute(value, axis, [(i, (i + by) % size) for i in range(size)])


def spread_kernel(zero_hbm, one_hbm, out_ref, zero_ref, one_ref, sems):
    loads = [
        pltpu.make_async_copy(zero_hbm, zero_ref, sems.at[0]),
        pltpu.make_async_copy(one_hbm, one_ref, sems.at[1]),
    ]
    for load in loads:
        load.start()
    for load in loads:
        load.wait()
    copies = out_ref.shape[0]
    at = 0
    for i in range(zero_ref.shape[0] // 8):
        for t in range(zero_ref.shape[1] // LANES):
            tile = zero_ref[8 * i : 8 * i + 8, t * LANES : (t + 1) * LANES]
            for k in range(copies):
                out_ref[k, at] = tile
            at += 1
    for p in range(one_ref.shape[1]):
        for i in range(one_ref.shape[0] // 8):
            for t in range(one_ref.shape[2] // LANES):
                tile = one_ref[8 * i : 8 * i + 8, p, t * LANES : (t + 1) * LANES]
                for k in range(copies):
                    out_ref[k, at] = tile
                at += 1


def spread(zero, one, copies):
    tiles = (zero.size + one.size) // (8 * LANES)
    vmem = pl.BlockSpec(memory_space=pltpu.VMEM)
    out = pl.pallas_call(
        spread_kernel,
        out_shape=jax.ShapeDtypeStruct((copies, tiles, 8, LANES), jnp.bfloat16),
        in_specs=[pl.BlockSpec(memory_space=pltpu.HBM)] * 2,
        out_specs=vmem,
        scratch_shapes=[
            pltpu.VMEM(zero.shape, zero.dtype),
            pltpu.VMEM(one.shape, one.dtype),
            pltpu.SemaphoreType.DMA((2,)),
        ],
        compiler_params=pltpu.CompilerParams(vmem_limit_bytes=8 * MIB),
        name="spread_weights",
    )(zero, one)
    return out.reshape(copies, tiles * 8, LANES)


def merge_kernel(factor_ref, chunk_ref, send_ref, other_ref, own_ref):
    zs, tiles = chunk_ref.shape[:2]
    targets = (
        (own_ref, [factor_ref[0, k] for k in range(zs)]),
        (send_ref.at[0], [factor_ref[1, k] for k in range(zs)]),
        (other_ref, [factor_ref[2, k] for k in range(zs)]),
        (send_ref.at[1], [factor_ref[3, k] for k in range(zs)]),
    )
    for j in range(tiles):
        pieces = [chunk_ref[k, j].astype(jnp.float32) for k in range(zs)]
        for ref, by in targets:
            total = by[0] * pieces[0]
            for k in range(1, zs):
                total = total + by[k] * pieces[k]
            ref[j] = total.astype(ref.dtype)


def partial_sums(factors, chunks):
    zs, rows, lanes = chunks.shape
    tiles = rows // 8
    one = jax.ShapeDtypeStruct((tiles, 8, lanes), jnp.bfloat16)
    vmem = pl.BlockSpec(memory_space=pltpu.VMEM)
    smem = pl.BlockSpec(memory_space=pltpu.SMEM)
    outs = pl.pallas_call(
        merge_kernel,
        out_shape=(jax.ShapeDtypeStruct((2, tiles, 8, lanes), jnp.bfloat16), one, one),
        in_specs=[smem, vmem],
        out_specs=(vmem, vmem, vmem),
        compiler_params=pltpu.CompilerParams(vmem_limit_bytes=12 * MIB),
        name="merge_experts",
    )(factors, chunks.reshape(zs, tiles, 8, lanes))
    return tuple(o.reshape(-1, rows, lanes) if o.ndim == 4 else o.reshape(rows, lanes) for o in outs)


def rotate_kernel(slot_ref, neighbour_ref, *refs):
    piece_refs = refs[:4]
    wigner_ref, out_ref, feature_ref, row_ref, spread_ref = refs[4:]
    frame = wigner_ref.shape[0]
    runs, harmonics = piece_refs[0].shape[:2]
    row_ref[:, 8 * harmonics :] = jnp.zeros_like(row_ref[:, 8 * harmonics :])

    def eight_atoms(run, carry):
        for k, ref in enumerate(piece_refs):
            row_ref[k, : 8 * harmonics] = ref[run].astype(jnp.float32).reshape(8 * harmonics, LANES)
            for a in range(8):
                rows = row_ref[k, a * harmonics : a * harmonics + PAD]
                feature_ref[(k * runs + run) * 8 + a] = rows.astype(jnp.bfloat16)
        return carry

    lax.fori_loop(0, runs, eight_atoms, 0)
    width = GROUP * PAD
    block = LANES
    column = lax.broadcasted_iota(jnp.int32, (PAD, width), 1)
    row = lax.broadcasted_iota(jnp.int32, (PAD, width), 0)
    repeat = (column % PAD == row).astype(jnp.bfloat16)
    edge = lax.broadcasted_iota(jnp.int32, (block, width), 0)
    lane = lax.broadcasted_iota(jnp.int32, (block, width), 1)
    own = edge % GROUP == lane // PAD

    def one_block(b, carry):
        start = pl.multiple_of(b * block, block)
        for r in range(frame):
            part = lax.dot_general(
                wigner_ref[r, :, pl.ds(start, block)],
                repeat,
                (((0,), (0,)), ((), ())),
                preferred_element_type=jnp.float32,
            )
            spread_ref[r] = jnp.where(own, part, 0.0)
        for pair in range(block // (2 * GROUP)):
            halves = []
            for half in range(2):
                low = (2 * pair + half) * GROUP
                tiles = []
                for e in range(GROUP):
                    source = slot_ref[neighbour_ref[start + low + e]]
                    tiles.append(feature_ref[source])
                stacked = jnp.concatenate(tiles, axis=0)
                rows = jnp.concatenate(
                    [spread_ref[r, low : low + GROUP, :] for r in range(frame)], axis=0
                ).astype(jnp.bfloat16)
                halves.append(
                    lax.dot_general(
                        rows, stacked, (((1,), (0,)), ((), ())), preferred_element_type=jnp.float32
                    )
                )
            for r in range(frame):
                both = jnp.concatenate([h[GROUP * r : GROUP * (r + 1)] for h in halves], axis=0)
                out_ref[
                    pl.ds(pl.multiple_of(start + 2 * GROUP * pair, 2 * GROUP), 2 * GROUP),
                    r * LANES : (r + 1) * LANES,
                ] = both.astype(out_ref.dtype)
        return carry

    lax.fori_loop(0, neighbour_ref.shape[0] // block, one_block, 0)


def rotate(slots, neighbour, pieces, wigner):
    frame, _, edges = wigner.shape
    runs, harmonics = pieces[0].shape[:2]
    atoms = len(pieces) * runs * 8
    return pl.pallas_call(
        rotate_kernel,
        out_shape=jax.ShapeDtypeStruct((edges, frame * LANES), jnp.bfloat16),
        in_specs=[
            pl.BlockSpec(memory_space=pltpu.SMEM),
            pl.BlockSpec(memory_space=pltpu.SMEM),
        ]
        + [pl.BlockSpec(memory_space=pltpu.VMEM)] * (len(pieces) + 1),
        out_specs=pl.BlockSpec(memory_space=pltpu.VMEM),
        scratch_shapes=[
            pltpu.VMEM((atoms, PAD, LANES), jnp.bfloat16),
            pltpu.VMEM((len(pieces), 8 * harmonics + 8, LANES), jnp.float32),
            pltpu.VMEM((frame, LANES, GROUP * PAD), jnp.float32),
        ],
        compiler_params=pltpu.CompilerParams(vmem_limit_bytes=20 * MIB),
        name="rotate_edges",
    )(slots, neighbour, *pieces, wigner)


def convolve_kernel(zero_shape, one_shape, x_ref, *refs):
    xs = 4
    column_refs = refs[:xs]
    rotated_ref, wigner_ref, out_ref, zero32, one32, zero16, real16, imag16, message, total = refs[xs:]
    zero_rows, zero_width = zero_shape
    parts, one_rows, one_width = one_shape
    ys = column_refs[0].shape[0]
    zero_tiles, one_tiles = zero_width // LANES, one_width // LANES
    for k in range(xs):
        place = (x_ref[1] + k) % xs
        for y in range(ys):
            g = (x_ref[0] + y) % ys * xs + place
            for i in range(zero_rows // 8):
                at = pl.multiple_of(g * zero_rows + 8 * i, 8)
                for t in range(zero_tiles):
                    zero32[pl.ds(at, 8), t * LANES : (t + 1) * LANES] = column_refs[k][
                        y, i * zero_tiles + t
                    ].astype(jnp.float32)
            first = zero_rows // 8 * zero_tiles
            for p in range(parts):
                for i in range(one_rows // 8):
                    at = pl.multiple_of(g * one_rows + 8 * i, 8)
                    for t in range(one_tiles):
                        one32[p, pl.ds(at, 8), t * LANES : (t + 1) * LANES] = column_refs[k][
                            y, first + (p * (one_rows // 8) + i) * one_tiles + t
                        ].astype(jnp.float32)
    zero16[...] = zero32[...].astype(jnp.bfloat16)
    real16[...] = one32[0].astype(jnp.bfloat16)
    imag16[...] = one32[1].astype(jnp.bfloat16)

    edges = rotated_ref.shape[0]
    frame = wigner_ref.shape[0]
    atoms = edges // NEIGH
    side = LMAX * LANES
    near = zero_width

    def times(a, b_ref):
        return lax.dot_general(a, b_ref[...], (((1,), (1,)), ((), ())), preferred_element_type=jnp.float32)

    rows = edges // 3
    for b in range(3):
        span = slice(b * rows, (b + 1) * rows)
        message[span, :near] = times(rotated_ref[span, :near], zero16).astype(jnp.bfloat16)
        plus = rotated_ref[span, near : near + side]
        minus = rotated_ref[span, near + side :]
        message[span, near : near + side] = (times(plus, real16) - times(minus, imag16)).astype(jnp.bfloat16)
        message[span, near + side :] = (times(plus, imag16) + times(minus, real16)).astype(jnp.bfloat16)

    total[...] = jnp.zeros_like(total)
    lane = lax.broadcasted_iota(jnp.int32, (PAD, LANES), 1)
    for b in range(edges // LANES):
        low = b * LANES
        first_atom = low // NEIGH
        last_atom = (low + LANES - 1) // NEIGH
        part = None
        for r0 in range(0, frame, 2):
            pair = [r for r in (r0, r0 + 1) if r < frame]
            left = []
            for r in pair:
                w = wigner_ref[r, :, low : low + LANES]
                picks = []
                for a in range(first_atom, last_atom + 1):
                    inside = (lane + low >= a * NEIGH) & (lane + low < (a + 1) * NEIGH)
                    picks.append(jnp.where(inside, w, jnp.zeros_like(w)))
                left.append(jnp.concatenate(picks, axis=0))
            lhs = jnp.concatenate(left, axis=1)
            rhs = jnp.concatenate(
                [message[low : low + LANES, r * LANES : (r + 1) * LANES] for r in pair], axis=0
            )
            got = lax.dot_general(lhs, rhs, (((1,), (0,)), ((), ())), preferred_element_type=jnp.float32)
            part = got if part is None else part + got
        window = slice(first_atom * PAD, (last_atom + 1) * PAD)
        total[window, :] = total[window, :] + part
    for k in range(out_ref.shape[0]):
        row = total[pl.ds(k, atoms, stride=PAD), :]
        out_ref[k] = (row * (1.0 / math.sqrt(NEIGH))).astype(out_ref.dtype)


def convolve(x, columns, rotated, wigner, zero_shape, one_shape, harmonics):
    edges = rotated.shape[0]
    atoms = edges // NEIGH
    parts, _, one_width = one_shape
    total_zero, total_one = zero_shape[1], one_width
    return pl.pallas_call(
        lambda *refs: convolve_kernel(zero_shape, one_shape, *refs),
        out_shape=jax.ShapeDtypeStruct((harmonics, atoms, LANES), jnp.bfloat16),
        in_specs=[pl.BlockSpec(memory_space=pltpu.SMEM)]
        + [pl.BlockSpec(memory_space=pltpu.VMEM)] * (len(columns) + 2),
        out_specs=pl.BlockSpec(memory_space=pltpu.VMEM),
        scratch_shapes=[
            pltpu.VMEM((total_zero, total_zero), jnp.float32),
            pltpu.VMEM((parts, total_one, total_one), jnp.float32),
            pltpu.VMEM((total_zero, total_zero), jnp.bfloat16),
            pltpu.VMEM((total_one, total_one), jnp.bfloat16),
            pltpu.VMEM((total_one, total_one), jnp.bfloat16),
            pltpu.VMEM((edges, rotated.shape[1]), jnp.bfloat16),
            pltpu.VMEM((atoms * PAD, LANES), jnp.float32),
        ],
        compiler_params=pltpu.CompilerParams(vmem_limit_bytes=28 * MIB),
        name="convolve_edges",
    )(x, *columns, rotated, wigner)


def added(a, b):
    return (a.astype(jnp.float32) + b.astype(jnp.float32)).astype(jnp.bfloat16)


def shards(
    node_features,
    atom_slot,
    neighbour,
    pad_mask,
    envelope,
    wigner_rows,
    mix_table,
    zero_weight,
    one_weight,
):
    yh, z, c = (lax.axis_index(a) for a in SYS)
    y, x = (lax.axis_index(a) for a in GRAPH)
    ys, xs = lax.axis_size("yl"), lax.axis_size("x")
    zero_rows, zero_width = zero_weight.shape[1:]
    one_rows, parts, one_width = one_weight.shape[1:]
    harmonics = wigner_rows.shape[2]
    copies = spread(zero_weight[0], one_weight[0], lax.axis_size("z"))
    chunks = lax.all_to_all(copies, "z", 0, 0, tiled=True)
    mine = node_features[0].reshape(-1, LANES)
    line = [mine]
    for k in range(1, ys):
        line.append(turned(mine, "yl", -k))
    line = jnp.concatenate(line, axis=0)
    plane = [line] * xs
    for k in FAR_FIRST:
        plane[k] = turned(line, "x", -k)

    edge_gate = envelope[0] * pad_mask[0].astype(jnp.float32)
    padding = ((0, 0), (0, PAD - harmonics), (0, 0))
    wigner = jnp.pad(wigner_rows[0], padding)
    gated = jnp.pad((wigner_rows[0].astype(jnp.float32) * edge_gate).astype(jnp.bfloat16), padding)
    slots = atom_slot[0]
    atoms = node_features.shape[1]
    slots = (
        (slots // atoms - x) % xs * (ys * atoms) + (slots // (xs * atoms) - y) % ys * atoms + slots % atoms
    )
    edges_from = neighbour[0]
    zs = lax.axis_size("z")
    table = mix_table.reshape(2, zs, 2, 2, zs, 2)
    table = lax.dynamic_slice(table, (0, z, 0, yh, 0, c), (2, 1, 2, 1, zs, 1)).reshape(2, 2, zs)
    table = jnp.where(yh == 0, table, table[::-1])
    factors = jnp.where(c == 0, table, table[:, ::-1]).reshape(4, zs)
    there = jnp.stack([y, x])
    wigner, gated, slots, edges_from, chunks, factors, there = lax.optimization_barrier(
        (wigner, gated, slots, edges_from, chunks, factors, there)
    )
    send, other, own = partial_sums(factors, chunks)
    swapped = turned(send, "c", 1)
    outgoing = added(other, swapped[1])
    arrived = turned(outgoing, "yh", 1)
    pieces = [p.reshape(-1, harmonics, 8, LANES) for p in plane]
    merged = added(added(own, swapped[0]), arrived)
    column = [merged]
    for k in range(1, ys):
        column.append(turned(merged, "yl", -k))
    column = jnp.stack(column)
    columns = [column] * xs
    for k in FAR_FIRST:
        columns[k] = turned(column, "x", -k)
    rotated = rotate(slots, edges_from, pieces, wigner)
    update = convolve(
        there,
        [m.reshape(ys, -1, 8, LANES) for m in columns],
        rotated,
        gated,
        (zero_rows, zero_width),
        (parts, one_rows, one_width),
        harmonics,
    )
    return update.transpose(1, 0, 2)[None]


def solution(mesh):
    finer = Mesh(mesh.devices.reshape(2, 8, 2, 4, 4), SYS + GRAPH)
    return jax.shard_map(
        shards,
        mesh=finer,
        in_specs=(
            P(SYS, GRAPH, None, None),
            P(SYS, None),
            P(SYS, GRAPH),
            P(SYS, GRAPH),
            P(SYS, GRAPH),
            P(SYS, None, None, GRAPH),
            P(),
            P(SYS, GRAPH, None),
            P(SYS, GRAPH, None, None),
        ),
        out_specs=P(SYS, GRAPH, None, None),
        check_vma=False,
    )
```

```python
import math

import jax
import jax.numpy as jnp
from jax import lax
from jax.experimental import pallas as pl
from jax.experimental.pallas import tpu as pltpu
from jax.sharding import Mesh
from jax.sharding import PartitionSpec as P


LMAX = 4
NEIGH = 72
SYS = ("yh", "z", "c")
GRAPH = ("yl", "x")
LANES = 128
PAD = 32
GROUP = 8
FAR_FIRST = (2, 1, 3)
MIB = 1024 * 1024


def turned(value, axis, by):
    size = lax.axis_size(axis)
    return lax.ppermute(value, axis, [(i, (i + by) % size) for i in range(size)])


def spread_kernel(zero_hbm, one_hbm, out_ref, zero_ref, one_ref, sems):
    loads = [
        pltpu.make_async_copy(zero_hbm, zero_ref, sems.at[0]),
        pltpu.make_async_copy(one_hbm, one_ref, sems.at[1]),
    ]
    for load in loads:
        load.start()
    for load in loads:
        load.wait()
    copies = out_ref.shape[0]
    at = 0
    for i in range(zero_ref.shape[0] // 8):
        for t in range(zero_ref.shape[1] // LANES):
            tile = zero_ref[8 * i : 8 * i + 8, t * LANES : (t + 1) * LANES]
            for k in range(copies):
                out_ref[k, at] = tile
            at += 1
    for p in range(one_ref.shape[1]):
        for i in range(one_ref.shape[0] // 8):
            for t in range(one_ref.shape[2] // LANES):
                tile = one_ref[8 * i : 8 * i + 8, p, t * LANES : (t + 1) * LANES]
                for k in range(copies):
                    out_ref[k, at] = tile
                at += 1


def spread(zero, one, copies):
    tiles = (zero.size + one.size) // (8 * LANES)
    vmem = pl.BlockSpec(memory_space=pltpu.VMEM)
    out = pl.pallas_call(
        spread_kernel,
        out_shape=jax.ShapeDtypeStruct((copies, tiles, 8, LANES), jnp.bfloat16),
        in_specs=[pl.BlockSpec(memory_space=pltpu.HBM)] * 2,
        out_specs=vmem,
        scratch_shapes=[
            pltpu.VMEM(zero.shape, zero.dtype),
            pltpu.VMEM(one.shape, one.dtype),
            pltpu.SemaphoreType.DMA((2,)),
        ],
        name="spread_weights",
    )(zero, one)
    return out.reshape(copies, tiles * 8, LANES)


def merge_kernel(factor_ref, chunk_ref, send_ref, other_ref, own_ref):
    zs, tiles = chunk_ref.shape[:2]
    targets = (
        (own_ref, [factor_ref[0, k] for k in range(zs)]),
        (send_ref.at[0], [factor_ref[1, k] for k in range(zs)]),
        (other_ref, [factor_ref[2, k] for k in range(zs)]),
        (send_ref.at[1], [factor_ref[3, k] for k in range(zs)]),
    )
    for j in range(tiles):
        pieces = [chunk_ref[k, j].astype(jnp.float32) for k in range(zs)]
        for ref, by in targets:
            total = by[0] * pieces[0]
            for k in range(1, zs):
                total = total + by[k] * pieces[k]
            ref[j] = total.astype(ref.dtype)


def partial_sums(factors, chunks):
    zs, rows, lanes = chunks.shape
    tiles = rows // 8
    one = jax.ShapeDtypeStruct((tiles, 8, lanes), jnp.bfloat16)
    vmem = pl.BlockSpec(memory_space=pltpu.VMEM)
    smem = pl.BlockSpec(memory_space=pltpu.SMEM)
    outs = pl.pallas_call(
        merge_kernel,
        out_shape=(jax.ShapeDtypeStruct((2, tiles, 8, lanes), jnp.bfloat16), one, one),
        in_specs=[smem, vmem],
        out_specs=(vmem, vmem, vmem),
        compiler_params=pltpu.CompilerParams(vmem_limit_bytes=12 * MIB),
        name="merge_experts",
    )(factors, chunks.reshape(zs, tiles, 8, lanes))
    return tuple(o.reshape(-1, rows, lanes) if o.ndim == 4 else o.reshape(rows, lanes) for o in outs)


def atoms_of(block):
    return block * LANES // NEIGH, ((block + 1) * LANES - 1) // NEIGH + 1


def pick_atoms(gated_ref, picked_ref):
    lane = lax.broadcasted_iota(jnp.int32, (PAD, LANES), 1)
    for b in range(picked_ref.shape[0]):
        low = b * LANES
        first, last = atoms_of(b)
        for r in range(gated_ref.shape[0]):
            w = gated_ref[r, :, low : low + LANES]
            for a in range(first, last):
                inside = (lane + low >= a * NEIGH) & (lane + low < (a + 1) * NEIGH)
                picked_ref[
                    b,
                    r // 2,
                    (a - first) * PAD : (a - first + 1) * PAD,
                    r % 2 * LANES : (r % 2 + 1) * LANES,
                ] = jnp.where(inside, w, jnp.zeros_like(w))


def rotate_kernel(slot_ref, neighbour_ref, *refs):
    piece_refs = refs[:4]
    wigner_ref, gated_ref, out_ref, picked_ref, feature_ref, row_ref, spread_ref = refs[4:]
    frame = wigner_ref.shape[0]
    pick_atoms(gated_ref, picked_ref)
    runs, harmonics = piece_refs[0].shape[:2]
    row_ref[:, 8 * harmonics :] = jnp.zeros_like(row_ref[:, 8 * harmonics :])

    def eight_atoms(run, carry):
        for k, ref in enumerate(piece_refs):
            row_ref[k, : 8 * harmonics] = ref[run].astype(jnp.float32).reshape(8 * harmonics, LANES)
            for a in range(8):
                rows = row_ref[k, a * harmonics : a * harmonics + PAD]
                feature_ref[(k * runs + run) * 8 + a] = rows.astype(jnp.bfloat16)
        return carry

    lax.fori_loop(0, runs, eight_atoms, 0)
    width = GROUP * PAD
    block = LANES
    column = lax.broadcasted_iota(jnp.int32, (PAD, width), 1)
    row = lax.broadcasted_iota(jnp.int32, (PAD, width), 0)
    repeat = (column % PAD == row).astype(jnp.bfloat16)
    edge = lax.broadcasted_iota(jnp.int32, (block, width), 0)
    lane = lax.broadcasted_iota(jnp.int32, (block, width), 1)
    own = edge % GROUP == lane // PAD

    def one_block(b, carry):
        start = pl.multiple_of(b * block, block)
        for r in range(frame):
            part = lax.dot_general(
                wigner_ref[r, :, pl.ds(start, block)],
                repeat,
                (((0,), (0,)), ((), ())),
                preferred_element_type=jnp.float32,
            )
            spread_ref[r] = jnp.where(own, part, 0.0)
        for pair in range(block // (2 * GROUP)):
            halves = []
            for half in range(2):
                low = (2 * pair + half) * GROUP
                tiles = []
                for e in range(GROUP):
                    source = slot_ref[neighbour_ref[start + low + e]]
                    tiles.append(feature_ref[source])
                stacked = jnp.concatenate(tiles, axis=0)
                rows = jnp.concatenate(
                    [spread_ref[r, low : low + GROUP, :] for r in range(frame)], axis=0
                ).astype(jnp.bfloat16)
                halves.append(
                    lax.dot_general(
                        rows, stacked, (((1,), (0,)), ((), ())), preferred_element_type=jnp.float32
                    )
                )
            rows = pl.ds(pl.multiple_of(start + 2 * GROUP * pair, 2 * GROUP), 2 * GROUP)
            both = []
            for r in range(frame):
                tile = jnp.concatenate([h[GROUP * r : GROUP * (r + 1)] for h in halves], axis=0)
                tile = tile.astype(out_ref.dtype)
                out_ref[rows, r * LANES : (r + 1) * LANES] = tile
                both.append(tile.astype(jnp.float32))
            for m in range(LMAX):
                tile = both[LMAX + 1 + m] + both[2 * LMAX + 1 + m]
                out_ref[rows, (frame + m) * LANES : (frame + m + 1) * LANES] = tile.astype(out_ref.dtype)
        return carry

    lax.fori_loop(0, neighbour_ref.shape[0] // block, one_block, 0)


def rotate(slots, neighbour, pieces, wigner, gated):
    frame, _, edges = wigner.shape
    runs, harmonics = pieces[0].shape[:2]
    atoms = len(pieces) * runs * 8
    return pl.pallas_call(
        rotate_kernel,
        out_shape=(
            jax.ShapeDtypeStruct((edges, (frame + LMAX) * LANES), jnp.bfloat16),
            jax.ShapeDtypeStruct((edges // LANES, (frame + 1) // 2, 3 * PAD, 2 * LANES), jnp.bfloat16),
        ),
        in_specs=[
            pl.BlockSpec(memory_space=pltpu.SMEM),
            pl.BlockSpec(memory_space=pltpu.SMEM),
        ]
        + [pl.BlockSpec(memory_space=pltpu.VMEM)] * (len(pieces) + 2),
        out_specs=(pl.BlockSpec(memory_space=pltpu.VMEM), pl.BlockSpec(memory_space=pltpu.VMEM)),
        scratch_shapes=[
            pltpu.VMEM((atoms, PAD, LANES), jnp.bfloat16),
            pltpu.VMEM((len(pieces), 8 * harmonics + 8, LANES), jnp.float32),
            pltpu.VMEM((frame, LANES, GROUP * PAD), jnp.float32),
        ],
        compiler_params=pltpu.CompilerParams(vmem_limit_bytes=26 * MIB),
        name="rotate_edges",
    )(slots, neighbour, *pieces, wigner, gated)


def convolve_kernel(zero_shape, one_shape, x_ref, *refs):
    xs = 4
    column_refs = refs[:xs]
    rotated_ref, picked_ref, out_ref, zero32, one32, zero16, real16, sum16, diff16, message, total = refs[xs:]
    zero_rows, zero_width = zero_shape
    parts, one_rows, one_width = one_shape
    ys = column_refs[0].shape[0]
    zero_tiles, one_tiles = zero_width // LANES, one_width // LANES
    for k in range(xs):
        place = (x_ref[1] + k) % xs
        for y in range(ys):
            g = (x_ref[0] + y) % ys * xs + place
            for i in range(zero_rows // 8):
                at = pl.multiple_of(g * zero_rows + 8 * i, 8)
                for t in range(zero_tiles):
                    zero32[pl.ds(at, 8), t * LANES : (t + 1) * LANES] = column_refs[k][
                        y, i * zero_tiles + t
                    ].astype(jnp.float32)
            first = zero_rows // 8 * zero_tiles
            for p in range(parts):
                for i in range(one_rows // 8):
                    at = pl.multiple_of(g * one_rows + 8 * i, 8)
                    for t in range(one_tiles):
                        one32[p, pl.ds(at, 8), t * LANES : (t + 1) * LANES] = column_refs[k][
                            y, first + (p * (one_rows // 8) + i) * one_tiles + t
                        ].astype(jnp.float32)
    zero16[...] = zero32[...].astype(jnp.bfloat16)
    real16[...] = one32[0].astype(jnp.bfloat16)
    sum16[...] = (one32[0] + one32[1]).astype(jnp.bfloat16)
    diff16[...] = (one32[1] - one32[0]).astype(jnp.bfloat16)

    edges = rotated_ref.shape[0]
    frame = 3 * LMAX + 1
    atoms = edges // NEIGH
    side = LMAX * LANES
    near = zero_width

    def times(a, b_ref):
        return lax.dot_general(a, b_ref[...], (((1,), (1,)), ((), ())), preferred_element_type=jnp.float32)

    rows = edges // 3
    for b in range(3):
        span = slice(b * rows, (b + 1) * rows)
        message[span, :near] = times(rotated_ref[span, :near], zero16).astype(jnp.bfloat16)
        plus = rotated_ref[span, near : near + side]
        minus = rotated_ref[span, near + side : near + 2 * side]
        shared = times(rotated_ref[span, near + 2 * side :], real16)
        message[span, near : near + side] = (shared - times(minus, sum16)).astype(jnp.bfloat16)
        message[span, near + side :] = (shared + times(plus, diff16)).astype(jnp.bfloat16)

    total[...] = jnp.zeros_like(total)
    for b in range(edges // LANES):
        low = b * LANES
        first, last = atoms_of(b)
        part = None
        for r0 in range(0, frame, 2):
            pair = [r for r in (r0, r0 + 1) if r < frame]
            lhs = picked_ref[b, r0 // 2, : (last - first) * PAD, : len(pair) * LANES]
            rhs = jnp.concatenate(
                [message[low : low + LANES, r * LANES : (r + 1) * LANES] for r in pair], axis=0
            )
            got = lax.dot_general(lhs, rhs, (((1,), (0,)), ((), ())), preferred_element_type=jnp.float32)
            part = got if part is None else part + got
        window = slice(first * PAD, last * PAD)
        total[window, :] = total[window, :] + part
    for k in range(out_ref.shape[0]):
        row = total[pl.ds(k, atoms, stride=PAD), :]
        out_ref[k] = (row * (1.0 / math.sqrt(NEIGH))).astype(out_ref.dtype)


def convolve(x, columns, rotated, picked, zero_shape, one_shape, harmonics):
    edges = rotated.shape[0]
    atoms = edges // NEIGH
    parts, _, one_width = one_shape
    total_zero, total_one = zero_shape[1], one_width
    return pl.pallas_call(
        lambda *refs: convolve_kernel(zero_shape, one_shape, *refs),
        out_shape=jax.ShapeDtypeStruct((harmonics, atoms, LANES), jnp.bfloat16),
        in_specs=[pl.BlockSpec(memory_space=pltpu.SMEM)]
        + [pl.BlockSpec(memory_space=pltpu.VMEM)] * (len(columns) + 2),
        out_specs=pl.BlockSpec(memory_space=pltpu.VMEM),
        scratch_shapes=[
            pltpu.VMEM((total_zero, total_zero), jnp.float32),
            pltpu.VMEM((parts, total_one, total_one), jnp.float32),
            pltpu.VMEM((total_zero, total_zero), jnp.bfloat16),
            pltpu.VMEM((total_one, total_one), jnp.bfloat16),
            pltpu.VMEM((total_one, total_one), jnp.bfloat16),
            pltpu.VMEM((total_one, total_one), jnp.bfloat16),
            pltpu.VMEM((edges, total_zero + parts * total_one), jnp.bfloat16),
            pltpu.VMEM((atoms * PAD, LANES), jnp.float32),
        ],
        compiler_params=pltpu.CompilerParams(vmem_limit_bytes=28 * MIB),
        name="convolve_edges",
    )(x, *columns, rotated, picked)


def added(a, b):
    return (a.astype(jnp.float32) + b.astype(jnp.float32)).astype(jnp.bfloat16)


def shards(
    node_features,
    atom_slot,
    neighbour,
    pad_mask,
    envelope,
    wigner_rows,
    mix_table,
    zero_weight,
    one_weight,
):
    yh, z, c = (lax.axis_index(a) for a in SYS)
    y, x = (lax.axis_index(a) for a in GRAPH)
    ys, xs = lax.axis_size("yl"), lax.axis_size("x")
    zero_rows, zero_width = zero_weight.shape[1:]
    one_rows, parts, one_width = one_weight.shape[1:]
    harmonics = wigner_rows.shape[2]
    copies = spread(zero_weight[0], one_weight[0], lax.axis_size("z"))
    chunks = lax.all_to_all(copies, "z", 0, 0, tiled=True)
    mine = node_features[0].reshape(-1, LANES)
    line = [mine]
    for k in range(1, ys):
        line.append(turned(mine, "yl", -k))
    line = jnp.concatenate(line, axis=0)
    plane = [line] * xs
    for k in FAR_FIRST:
        plane[k] = turned(line, "x", -k)

    edge_gate = envelope[0] * pad_mask[0].astype(jnp.float32)
    padding = ((0, 0), (0, PAD - harmonics), (0, 0))
    wigner = jnp.pad(wigner_rows[0], padding)
    gated = jnp.pad((wigner_rows[0].astype(jnp.float32) * edge_gate).astype(jnp.bfloat16), padding)
    slots = atom_slot[0]
    atoms = node_features.shape[1]
    slots = (
        (slots // atoms - x) % xs * (ys * atoms) + (slots // (xs * atoms) - y) % ys * atoms + slots % atoms
    )
    edges_from = neighbour[0]
    zs = lax.axis_size("z")
    table = mix_table.reshape(2, zs, 2, 2, zs, 2)
    table = lax.dynamic_slice(table, (0, z, 0, yh, 0, c), (2, 1, 2, 1, zs, 1)).reshape(2, 2, zs)
    table = jnp.where(yh == 0, table, table[::-1])
    factors = jnp.where(c == 0, table, table[:, ::-1]).reshape(4, zs)
    there = jnp.stack([y, x])
    wigner, gated, slots, edges_from, chunks, factors, there = lax.optimization_barrier(
        (wigner, gated, slots, edges_from, chunks, factors, there)
    )
    send, other, own = partial_sums(factors, chunks)
    swapped = turned(send, "c", 1)
    outgoing = added(other, swapped[1])
    arrived = turned(outgoing, "yh", 1)
    pieces = [p.reshape(-1, harmonics, 8, LANES) for p in plane]
    merged = added(added(own, swapped[0]), arrived)
    column = [merged]
    for k in range(1, ys):
        column.append(turned(merged, "yl", -k))
    column = jnp.stack(column)
    columns = [column] * xs
    for k in FAR_FIRST:
        columns[k] = turned(column, "x", -k)
    rotated, gathered = rotate(slots, edges_from, pieces, wigner, gated)
    update = convolve(
        there,
        [m.reshape(ys, -1, 8, LANES) for m in columns],
        rotated,
        gathered,
        (zero_rows, zero_width),
        (parts, one_rows, one_width),
        harmonics,
    )
    return update.transpose(1, 0, 2)[None]


def solution(mesh):
    finer = Mesh(mesh.devices.reshape(2, 8, 2, 4, 4), SYS + GRAPH)
    return jax.shard_map(
        shards,
        mesh=finer,
        in_specs=(
            P(SYS, GRAPH, None, None),
            P(SYS, None),
            P(SYS, GRAPH),
            P(SYS, GRAPH),
            P(SYS, GRAPH),
            P(SYS, None, None, GRAPH),
            P(),
            P(SYS, GRAPH, None),
            P(SYS, GRAPH, None, None),
        ),
        out_specs=P(SYS, GRAPH, None, None),
        check_vma=False,
    )
```

```python
import math

import jax
import jax.numpy as jnp
from jax import lax
from jax.experimental import pallas as pl
from jax.experimental.pallas import tpu as pltpu
from jax.sharding import Mesh
from jax.sharding import PartitionSpec as P


LMAX = 4
NEIGH = 72
SYS = ("yh", "z", "c")
GRAPH = ("yl", "x")
LANES = 128
PAD = 32
GROUP = 8
FAR_FIRST = (2, 1, 3)
MIB = 1024 * 1024


def turned(value, axis, by):
    size = lax.axis_size(axis)
    return lax.ppermute(value, axis, [(i, (i + by) % size) for i in range(size)])


def spread_kernel(zero_hbm, one_hbm, out_ref, zero_ref, one_ref, sems):
    loads = [
        pltpu.make_async_copy(zero_hbm, zero_ref, sems.at[0]),
        pltpu.make_async_copy(one_hbm, one_ref, sems.at[1]),
    ]
    for load in loads:
        load.start()
    for load in loads:
        load.wait()
    copies = out_ref.shape[0]
    at = 0
    for i in range(zero_ref.shape[0] // 8):
        for t in range(zero_ref.shape[1] // LANES):
            tile = zero_ref[8 * i : 8 * i + 8, t * LANES : (t + 1) * LANES]
            for k in range(copies):
                out_ref[k, at] = tile
            at += 1
    for p in range(one_ref.shape[1]):
        for i in range(one_ref.shape[0] // 8):
            for t in range(one_ref.shape[2] // LANES):
                tile = one_ref[8 * i : 8 * i + 8, p, t * LANES : (t + 1) * LANES]
                for k in range(copies):
                    out_ref[k, at] = tile
                at += 1


def spread(zero, one, copies):
    tiles = (zero.size + one.size) // (8 * LANES)
    vmem = pl.BlockSpec(memory_space=pltpu.VMEM)
    out = pl.pallas_call(
        spread_kernel,
        out_shape=jax.ShapeDtypeStruct((copies, tiles, 8, LANES), jnp.bfloat16),
        in_specs=[pl.BlockSpec(memory_space=pltpu.HBM)] * 2,
        out_specs=vmem,
        scratch_shapes=[
            pltpu.VMEM(zero.shape, zero.dtype),
            pltpu.VMEM(one.shape, one.dtype),
            pltpu.SemaphoreType.DMA((2,)),
        ],
        name="spread_weights",
    )(zero, one)
    return out.reshape(copies, tiles * 8, LANES)


def merge_kernel(factor_ref, chunk_ref, send_ref, other_ref, own_ref):
    zs, tiles = chunk_ref.shape[:2]
    targets = (
        (own_ref, [factor_ref[0, k] for k in range(zs)]),
        (send_ref.at[0], [factor_ref[1, k] for k in range(zs)]),
        (other_ref, [factor_ref[2, k] for k in range(zs)]),
        (send_ref.at[1], [factor_ref[3, k] for k in range(zs)]),
    )
    for j in range(tiles):
        pieces = [chunk_ref[k, j].astype(jnp.float32) for k in range(zs)]
        for ref, by in targets:
            total = by[0] * pieces[0]
            for k in range(1, zs):
                total = total + by[k] * pieces[k]
            ref[j] = total.astype(ref.dtype)


def partial_sums(factors, chunks):
    zs, rows, lanes = chunks.shape
    tiles = rows // 8
    one = jax.ShapeDtypeStruct((tiles, 8, lanes), jnp.bfloat16)
    vmem = pl.BlockSpec(memory_space=pltpu.VMEM)
    smem = pl.BlockSpec(memory_space=pltpu.SMEM)
    outs = pl.pallas_call(
        merge_kernel,
        out_shape=(jax.ShapeDtypeStruct((2, tiles, 8, lanes), jnp.bfloat16), one, one),
        in_specs=[smem, vmem],
        out_specs=(vmem, vmem, vmem),
        compiler_params=pltpu.CompilerParams(vmem_limit_bytes=12 * MIB),
        name="merge_experts",
    )(factors, chunks.reshape(zs, tiles, 8, lanes))
    return tuple(o.reshape(-1, rows, lanes) if o.ndim == 4 else o.reshape(rows, lanes) for o in outs)


def atoms_of(block):
    return block * LANES // NEIGH, ((block + 1) * LANES - 1) // NEIGH + 1


def pick_atoms(gated_ref, picked_ref):
    lane = lax.broadcasted_iota(jnp.int32, (PAD, LANES), 1)
    for b in range(picked_ref.shape[0]):
        low = b * LANES
        first, last = atoms_of(b)
        for r in range(gated_ref.shape[0]):
            w = gated_ref[r, :, low : low + LANES]
            for a in range(first, last):
                inside = (lane + low >= a * NEIGH) & (lane + low < (a + 1) * NEIGH)
                picked_ref[
                    b,
                    r // 2,
                    (a - first) * PAD : (a - first + 1) * PAD,
                    r % 2 * LANES : (r % 2 + 1) * LANES,
                ] = jnp.where(inside, w, jnp.zeros_like(w))


def frames_kernel(wigner_ref, rows_ref):
    frame = wigner_ref.shape[0]
    width = GROUP * PAD
    block = wigner_ref.shape[2]
    column = lax.broadcasted_iota(jnp.int32, (PAD, width), 1)
    row = lax.broadcasted_iota(jnp.int32, (PAD, width), 0)
    repeat = (column % PAD == row).astype(jnp.bfloat16)
    edge = lax.broadcasted_iota(jnp.int32, (block, width), 0)
    lane = lax.broadcasted_iota(jnp.int32, (block, width), 1)
    own = edge % GROUP == lane // PAD
    for r0 in range(0, frame, 2):
        parts = []
        for r in range(r0, min(r0 + 2, frame)):
            part = lax.dot_general(
                wigner_ref[r],
                repeat,
                (((0,), (0,)), ((), ())),
                preferred_element_type=jnp.float32,
            )
            parts.append(jnp.where(own, part, 0.0))
        for g in range(block // GROUP):
            low = g * GROUP
            tiles = [p[low : low + GROUP] for p in parts]
            tile = tiles[0] if len(tiles) == 1 else jnp.concatenate(tiles, axis=0)
            rows_ref[g, r0 * GROUP : r0 * GROUP + tile.shape[0]] = tile.astype(jnp.bfloat16)


def frames(wigner):
    frame, pad, edges = wigner.shape
    return pl.pallas_call(
        frames_kernel,
        grid=(edges // LANES,),
        out_shape=jax.ShapeDtypeStruct((edges // GROUP, frame * GROUP, GROUP * PAD), jnp.bfloat16),
        in_specs=[pl.BlockSpec((frame, pad, LANES), lambda b: (0, 0, b))],
        out_specs=pl.BlockSpec((LANES // GROUP, frame * GROUP, GROUP * PAD), lambda b: (b, 0, 0)),
        name="spread_frames",
    )(wigner)


def rotate_kernel(slot_ref, neighbour_ref, *refs):
    piece_refs = refs[:4]
    gated_ref, rows_ref, out_ref, picked_ref, feature_ref, row_ref = refs[4:]
    step = pl.program_id(0)
    frame = rows_ref.shape[1] // GROUP
    runs, harmonics = piece_refs[0].shape[:2]

    def eight_atoms(run, carry):
        for k, ref in enumerate(piece_refs):
            row_ref[k, : 8 * harmonics] = ref[run].astype(jnp.float32).reshape(8 * harmonics, LANES)
            for a in range(8):
                rows = row_ref[k, a * harmonics : a * harmonics + PAD]
                feature_ref[(k * runs + run) * 8 + a] = rows.astype(jnp.bfloat16)
        return carry

    @pl.when(step == 0)
    def _():
        pick_atoms(gated_ref, picked_ref)
        row_ref[:, 8 * harmonics :] = jnp.zeros_like(row_ref[:, 8 * harmonics :])
        lax.fori_loop(0, runs, eight_atoms, 0)

    for pair in range(rows_ref.shape[0] // 2):
        low = pair * 2 * GROUP
        start = step * LANES + low
        halves = []
        for half in range(2):
            tiles = []
            for e in range(GROUP):
                source = slot_ref[neighbour_ref[start + half * GROUP + e]]
                tiles.append(feature_ref[source])
            halves.append(
                lax.dot_general(
                    rows_ref[2 * pair + half],
                    jnp.concatenate(tiles, axis=0),
                    (((1,), (0,)), ((), ())),
                    preferred_element_type=jnp.float32,
                )
            )
        rows = slice(low, low + 2 * GROUP)
        both = []
        for r in range(frame):
            tile = jnp.concatenate([h[GROUP * r : GROUP * (r + 1)] for h in halves], axis=0)
            tile = tile.astype(out_ref.dtype)
            out_ref[rows, r * LANES : (r + 1) * LANES] = tile
            both.append(tile.astype(jnp.float32))
        for m in range(LMAX):
            tile = both[LMAX + 1 + m] + both[2 * LMAX + 1 + m]
            out_ref[rows, (frame + m) * LANES : (frame + m + 1) * LANES] = tile.astype(out_ref.dtype)


def rotate(slots, neighbour, pieces, gated, rows):
    frame = rows.shape[1] // GROUP
    edges = neighbour.shape[0]
    runs, harmonics = pieces[0].shape[:2]
    atoms = len(pieces) * runs * 8
    return pl.pallas_call(
        rotate_kernel,
        grid=(edges // LANES,),
        out_shape=(
            jax.ShapeDtypeStruct((edges, (frame + LMAX) * LANES), jnp.bfloat16),
            jax.ShapeDtypeStruct((edges // LANES, (frame + 1) // 2, 3 * PAD, 2 * LANES), jnp.bfloat16),
        ),
        in_specs=[
            pl.BlockSpec(memory_space=pltpu.SMEM),
            pl.BlockSpec(memory_space=pltpu.SMEM),
        ]
        + [pl.BlockSpec(memory_space=pltpu.VMEM)] * (len(pieces) + 1)
        + [pl.BlockSpec((LANES // GROUP, *rows.shape[1:]), lambda b: (b, 0, 0))],
        out_specs=(
            pl.BlockSpec((LANES, (frame + LMAX) * LANES), lambda b: (b, 0)),
            pl.BlockSpec(memory_space=pltpu.VMEM),
        ),
        scratch_shapes=[
            pltpu.VMEM((atoms, PAD, LANES), jnp.bfloat16),
            pltpu.VMEM((len(pieces), 8 * harmonics + 8, LANES), jnp.float32),
        ],
        compiler_params=pltpu.CompilerParams(vmem_limit_bytes=40 * MIB),
        name="rotate_edges",
    )(slots, neighbour, *pieces, gated, rows)


def convolve_kernel(zero_shape, one_shape, x_ref, *refs):
    xs = 4
    column_refs = refs[: 2 * xs]
    rotated_ref, picked_ref, out_ref, zero32, one32, zero16, real16, sum16, diff16, message, total = refs[2 * xs :]
    zero_rows, zero_width = zero_shape
    parts, one_rows, one_width = one_shape
    half = column_refs[0].shape[0]
    ys = 2 * half
    zero_tiles, one_tiles = zero_width // LANES, one_width // LANES
    for k in range(xs):
        place = (x_ref[1] + k) % xs
        for y in range(ys):
            g = (x_ref[0] + y) % ys * xs + place
            piece_ref = column_refs[2 * k + y // half].at[y % half]
            for i in range(zero_rows // 8):
                at = pl.multiple_of(g * zero_rows + 8 * i, 8)
                for t in range(zero_tiles):
                    zero32[pl.ds(at, 8), t * LANES : (t + 1) * LANES] = piece_ref[
                        i * zero_tiles + t
                    ].astype(jnp.float32)
            first = zero_rows // 8 * zero_tiles
            for p in range(parts):
                for i in range(one_rows // 8):
                    at = pl.multiple_of(g * one_rows + 8 * i, 8)
                    for t in range(one_tiles):
                        one32[p, pl.ds(at, 8), t * LANES : (t + 1) * LANES] = piece_ref[
                            first + (p * (one_rows // 8) + i) * one_tiles + t
                        ].astype(jnp.float32)
    zero16[...] = zero32[...].astype(jnp.bfloat16)
    real16[...] = one32[0].astype(jnp.bfloat16)
    sum16[...] = (one32[0] + one32[1]).astype(jnp.bfloat16)
    diff16[...] = (one32[1] - one32[0]).astype(jnp.bfloat16)

    edges = rotated_ref.shape[0]
    frame = 3 * LMAX + 1
    atoms = edges // NEIGH
    side = LMAX * LANES
    near = zero_width

    def times(a, b_ref):
        return lax.dot_general(a, b_ref[...], (((1,), (1,)), ((), ())), preferred_element_type=jnp.float32)

    rows = edges // 3
    for b in range(3):
        span = slice(b * rows, (b + 1) * rows)
        message[span, :near] = times(rotated_ref[span, :near], zero16).astype(jnp.bfloat16)
        plus = rotated_ref[span, near : near + side]
        minus = rotated_ref[span, near + side : near + 2 * side]
        shared = times(rotated_ref[span, near + 2 * side :], real16)
        message[span, near : near + side] = (shared - times(minus, sum16)).astype(jnp.bfloat16)
        message[span, near + side :] = (shared + times(plus, diff16)).astype(jnp.bfloat16)

    total[...] = jnp.zeros_like(total)
    for b in range(edges // LANES):
        low = b * LANES
        first, last = atoms_of(b)
        part = None
        for r0 in range(0, frame, 2):
            pair = [r for r in (r0, r0 + 1) if r < frame]
            lhs = picked_ref[b, r0 // 2, : (last - first) * PAD, : len(pair) * LANES]
            rhs = jnp.concatenate(
                [message[low : low + LANES, r * LANES : (r + 1) * LANES] for r in pair], axis=0
            )
            got = lax.dot_general(lhs, rhs, (((1,), (0,)), ((), ())), preferred_element_type=jnp.float32)
            part = got if part is None else part + got
        window = slice(first * PAD, last * PAD)
        total[window, :] = total[window, :] + part
    for k in range(out_ref.shape[0]):
        row = total[pl.ds(k, atoms, stride=PAD), :]
        out_ref[k] = (row * (1.0 / math.sqrt(NEIGH))).astype(out_ref.dtype)


def convolve(x, columns, rotated, picked, zero_shape, one_shape, harmonics):
    edges = rotated.shape[0]
    atoms = edges // NEIGH
    parts, _, one_width = one_shape
    total_zero, total_one = zero_shape[1], one_width
    return pl.pallas_call(
        lambda *refs: convolve_kernel(zero_shape, one_shape, *refs),
        out_shape=jax.ShapeDtypeStruct((harmonics, atoms, LANES), jnp.bfloat16),
        in_specs=[pl.BlockSpec(memory_space=pltpu.SMEM)]
        + [pl.BlockSpec(memory_space=pltpu.VMEM)] * (len(columns) + 2),
        out_specs=pl.BlockSpec(memory_space=pltpu.VMEM),
        scratch_shapes=[
            pltpu.VMEM((total_zero, total_zero), jnp.float32),
            pltpu.VMEM((parts, total_one, total_one), jnp.float32),
            pltpu.VMEM((total_zero, total_zero), jnp.bfloat16),
            pltpu.VMEM((total_one, total_one), jnp.bfloat16),
            pltpu.VMEM((total_one, total_one), jnp.bfloat16),
            pltpu.VMEM((total_one, total_one), jnp.bfloat16),
            pltpu.VMEM((edges, total_zero + parts * total_one), jnp.bfloat16),
            pltpu.VMEM((atoms * PAD, LANES), jnp.float32),
        ],
        compiler_params=pltpu.CompilerParams(vmem_limit_bytes=28 * MIB),
        name="convolve_edges",
    )(x, *columns, rotated, picked)


def added(a, b):
    return (a.astype(jnp.float32) + b.astype(jnp.float32)).astype(jnp.bfloat16)


def shards(
    node_features,
    atom_slot,
    neighbour,
    pad_mask,
    envelope,
    wigner_rows,
    mix_table,
    zero_weight,
    one_weight,
):
    yh, z, c = (lax.axis_index(a) for a in SYS)
    y, x = (lax.axis_index(a) for a in GRAPH)
    ys, xs = lax.axis_size("yl"), lax.axis_size("x")
    zero_rows, zero_width = zero_weight.shape[1:]
    one_rows, parts, one_width = one_weight.shape[1:]
    harmonics = wigner_rows.shape[2]
    copies = spread(zero_weight[0], one_weight[0], lax.axis_size("z"))
    chunks = lax.all_to_all(copies, "z", 0, 0, tiled=True)
    mine = node_features[0].reshape(-1, LANES)
    line = [mine]
    for k in range(1, ys):
        line.append(turned(mine, "yl", -k))
    line = jnp.concatenate(line, axis=0)
    plane = [line] * xs
    for k in FAR_FIRST:
        plane[k] = turned(line, "x", -k)

    edge_gate = envelope[0] * pad_mask[0].astype(jnp.float32)
    padding = ((0, 0), (0, PAD - harmonics), (0, 0))
    wigner = jnp.pad(wigner_rows[0], padding)
    gated = jnp.pad((wigner_rows[0].astype(jnp.float32) * edge_gate).astype(jnp.bfloat16), padding)
    slots = atom_slot[0]
    atoms = node_features.shape[1]
    slots = (
        (slots // atoms - x) % xs * (ys * atoms) + (slots // (xs * atoms) - y) % ys * atoms + slots % atoms
    )
    edges_from = neighbour[0]
    zs = lax.axis_size("z")
    table = mix_table.reshape(2, zs, 2, 2, zs, 2)
    table = lax.dynamic_slice(table, (0, z, 0, yh, 0, c), (2, 1, 2, 1, zs, 1)).reshape(2, 2, zs)
    table = jnp.where(yh == 0, table, table[::-1])
    factors = jnp.where(c == 0, table, table[:, ::-1]).reshape(4, zs)
    there = jnp.stack([y, x])
    rows = frames(wigner)
    rows, gated, slots, edges_from, chunks, factors, there = lax.optimization_barrier(
        (rows, gated, slots, edges_from, chunks, factors, there)
    )
    send, other, own = partial_sums(factors, chunks)
    swapped = turned(send, "c", 1)
    outgoing = added(other, swapped[1])
    arrived = turned(outgoing, "yh", 1)
    pieces = [p.reshape(-1, harmonics, 8, LANES) for p in plane]
    merged = added(added(own, swapped[0]), arrived)
    column = [merged]
    for k in range(1, ys):
        column.append(turned(merged, "yl", -k))
    halves = [jnp.stack(column[: ys // 2]), jnp.stack(column[ys // 2 :])]
    columns = {(0, half): rows for half, rows in enumerate(halves)}
    for half, by in ((0, 1), (0, 3), (1, 3), (1, 1)):
        columns[by, half] = turned(halves[half], "x", -by)
    for half, by in ((0, 1), (1, 3)):
        columns[2, half] = turned(columns[by, half], "x", -by)
    columns = [columns[k, half] for k in range(xs) for half in range(2)]
    rotated, gathered = rotate(slots, edges_from, pieces, gated, rows)
    update = convolve(
        there,
        [m.reshape(ys // 2, -1, 8, LANES) for m in columns],
        rotated,
        gathered,
        (zero_rows, zero_width),
        (parts, one_rows, one_width),
        harmonics,
    )
    return update.transpose(1, 0, 2)[None]


def solution(mesh):
    finer = Mesh(mesh.devices.reshape(2, 8, 2, 4, 4), SYS + GRAPH)
    return jax.shard_map(
        shards,
        mesh=finer,
        in_specs=(
            P(SYS, GRAPH, None, None),
            P(SYS, None),
            P(SYS, GRAPH),
            P(SYS, GRAPH),
            P(SYS, GRAPH),
            P(SYS, None, None, GRAPH),
            P(),
            P(SYS, GRAPH, None),
            P(SYS, GRAPH, None, None),
        ),
        out_specs=P(SYS, GRAPH, None, None),
        check_vma=False,
    )
```
